32 devices in a mesh: grp: 4 (over y, x), rep: 8 (over z, core).
Axes of the slice: x: 2, y: 2, z: 4, core: 2. Of those that a mesh axis runs over, the one named last changes fastest.
Arguments:
- activations: float32 [8, 1024, 2304], P('rep', 'grp'), may hold values from -250 to 250
- positions: int32 [8, 1024], P('rep'), may hold values from 0 to 1023, each once within a row
- w_qkv: bfloat16 [2304, 4096], P('grp'), may hold values from -11 to 11
- w_out: bfloat16 [2048, 2304], P('grp'), may hold values from -0.125 to 0.125
- w_in: bfloat16 [2304, 9216], P('grp'), may hold values from -0.125 to 0.125
- w_down: bfloat16 [4608, 2304], P('grp'), may hold values from -0.09375 to 0.09375
- gain_attn_in: bfloat16 [2304], P('grp'), may hold values from 0.25 to 1.75
- gain_attn_out: bfloat16 [2304], P('grp'), may hold values from 0.25 to 1.75
- gain_ffn_in: bfloat16 [2304], P('grp'), may hold values from 0.25 to 1.75
- gain_ffn_out: bfloat16 [2304], P('grp'), may hold values from 0.25 to 2.5
- cotangent: float32 [8, 1024, 2304], P('rep', 'grp'), may hold values from -6 to 6
Outputs:
- block_output: float32 [8, 1024, 2304], P('rep', 'grp')
- d_activations: float32 [8, 1024, 2304], P('rep', 'grp')
- d_w_qkv: float32 [2304, 4096], P('grp')
- d_w_out: float32 [2048, 2304], P('grp')
- d_w_in: float32 [2304, 9216], P('grp')
- d_w_down: float32 [4608, 2304], P('grp')
- d_gain_attn_in: float32 [2304], P('grp')
- d_gain_attn_out: float32 [2304], P('grp')
- d_gain_ffn_in: float32 [2304], P('grp')
- d_gain_ffn_out: float32 [2304], P('grp')
The draws below stay inside these ranges and needn't reach their ends.
All inputs are finite; a program needn't handle non-finite values.
Results may differ from the reference program's by a relative error of at most 0.023.
The reference program's roundings to bfloat16 on the way count: a program that leaves them out, or rounds other values in their place, can miss the bound.
Values may be sent and summed in bfloat16 or wider, within the bound.
No kernel may reach another device: no remote copies, remote signals or barrier semaphores. Data moves between devices by JAX's collectives and lax.ppermute only.
A program may use at most 512 MiB of HBM per device.

```python
import math
import jax
import jax.numpy as jnp
from jax import lax

D = 2304
QUERY_HEADS = 8
KEY_VALUE_HEADS = 4
HEAD_SIZE = 256
FF = 4608
SEQUENCE_LENGTH = 1024
QW = 2048
KW = 1024
BATCH = 8


def draw_activations(key, part):
    key_rows, key_cols, key_base = jax.random.split(key, 3)
    row_scale = jnp.exp(jax.random.uniform(key_rows, (BATCH, SEQUENCE_LENGTH, 1), jnp.float32, 0.0, math.log(10.0)))
    col_scale = jnp.exp(jax.random.uniform(key_cols, (1, 1, D), jnp.float32, math.log(0.5), math.log(5.0)))
    base = jnp.clip(jax.random.normal(key_base, (BATCH, SEQUENCE_LENGTH, D), jnp.float32), -5.0, 5.0)
    return (base * row_scale * col_scale).astype(jnp.float32)


def draw_w_qkv(key, part):
    key_base, key_order, key_jitter = jax.random.split(key, 3)
    columns_all = QW + 2 * KW
    base = jnp.clip(jax.random.normal(key_base, (D, columns_all), jnp.float32), -5.0, 5.0)
    order = jax.random.permutation(key_order, QUERY_HEADS).astype(jnp.float32)
    jitter = jax.random.uniform(key_jitter, (QUERY_HEADS,), jnp.float32)
    head_scale = jnp.exp(math.log(24.0) * (order + jitter) / QUERY_HEADS)
    col_scale = jnp.concatenate([jnp.repeat(head_scale, HEAD_SIZE), jnp.ones((2 * KW,), jnp.float32)])
    return (base * col_scale[None, :] / math.sqrt(D)).astype(jnp.bfloat16)


def steps_of(rng, shape, pieces, least, top_value):
    gain = 1.0
    for axis_at, parts in pieces:
        steps = jax.random.uniform(jax.random.fold_in(jax.random.fold_in(rng, 6), axis_at), (parts,), jnp.float32, least / len(pieces), top_value / len(pieces))
        gain = gain * jnp.repeat(jnp.exp(steps), shape[axis_at] // parts).reshape((-1,) + (1,) * (len(shape) - 1 - axis_at))
    return gain


def centred(own_key, dims, scale, most, cuts=(), held_as=jnp.bfloat16):
    loudness = steps_of(own_key, dims, cuts, -0.22, 0.18) if cuts else 1.0
    entries = jax.random.normal(own_key, dims, jnp.float32) * scale * loudness
    return jnp.minimum(jnp.maximum(entries, -most), most).astype(held_as)


def setup_inputs(seed: int = 0) -> dict:
    streams_of = jax.random.split(jax.random.key(seed), 12)
    activations = draw_activations(jax.random.fold_in(streams_of[11], 71), 0)
    positions = jax.vmap(lambda own: jax.random.permutation(own, SEQUENCE_LENGTH))(jax.random.split(streams_of[1], BATCH)).reshape((BATCH, SEQUENCE_LENGTH)).astype(jnp.int32)
    w_qkv = draw_w_qkv(jax.random.fold_in(streams_of[11], 71), 0)
    w_out = centred(streams_of[3], (QW, D), QW ** -0.5, 0.125, ((0, 4),))
    w_in = centred(streams_of[4], (D, 2 * FF), D ** -0.5, 0.125, ((0, 4),))
    w_down = centred(streams_of[5], (FF, D), FF ** -0.5, 0.09375, ((0, 4),))
    gain_attn_in = jnp.clip(1.0 + 0.15 * jax.random.normal(streams_of[6], (D,), jnp.float32), 0.25, 1.75).astype(jnp.bfloat16)
    gain_attn_out = jnp.clip(1.0 + 0.15 * jax.random.normal(streams_of[7], (D,), jnp.float32), 0.25, 1.75).astype(jnp.bfloat16)
    gain_ffn_in = jnp.clip(1.0 + 0.15 * jax.random.normal(streams_of[8], (D,), jnp.float32), 0.25, 1.75).astype(jnp.bfloat16)
    gain_ffn_out = jnp.clip(jnp.exp(math.log(2.5) - 2.3025851 * jax.random.uniform(streams_of[9], (D,), jnp.float32) ** steps_of(streams_of[9], (D,), ((0, 4),), -0.2, 0.2)), 0.25, 2.5).astype(jnp.bfloat16)
    cotangent = centred(streams_of[10], (BATCH, SEQUENCE_LENGTH, D), 1.0, 6.0, ((0, 8), (1, 4)), jnp.float32)
    return dict(activations=activations, positions=positions, w_qkv=w_qkv, w_out=w_out, w_in=w_in, w_down=w_down, gain_attn_in=gain_attn_in, gain_attn_out=gain_attn_out, gain_ffn_in=gain_ffn_in, gain_ffn_out=gain_ffn_out, cotangent=cotangent)


EPS = 1e-06
CAP = 50.0
GELU_C = math.sqrt(2.0 / math.pi)

def rms_scale(v):
    return lax.rsqrt(lax.optimization_barrier(jnp.mean(v * v, axis=-1, keepdims=True)) + EPS)

def norm_back(grad_n, normed, scale):
    return scale * (grad_n - normed * lax.optimization_barrier(jnp.mean(grad_n * normed, axis=-1, keepdims=True)))

def gelu_value(v):
    inner = GELU_C * (v + 0.044715 * v * v * v)
    return 0.5 * v * (1.0 + jnp.tanh(inner))

def gelu_slope(v):
    inner = GELU_C * (v + 0.044715 * v * v * v)
    tanh_val = jnp.tanh(inner)
    return 0.5 * (1.0 + tanh_val) + 0.5 * v * (1.0 - tanh_val * tanh_val) * GELU_C * (1.0 + 3.0 * 0.044715 * v * v)

def fdot(a, b):
    return jnp.dot(a, b, preferred_element_type=jnp.float32)

def reference(activations, positions, w_qkv, w_out, w_in, w_down, gain_attn_in, gain_attn_out, gain_ffn_in, gain_ffn_out, cotangent):
    query_width = QUERY_HEADS * HEAD_SIZE
    key_width = KEY_VALUE_HEADS * HEAD_SIZE
    group_share = QUERY_HEADS // KEY_VALUE_HEADS
    qscale = 1.0 / math.sqrt(HEAD_SIZE)
    gain_one = gain_attn_in.astype(jnp.float32)
    gain_two = gain_attn_out.astype(jnp.float32)
    gain_three = gain_ffn_in.astype(jnp.float32)
    gain_four = gain_ffn_out.astype(jnp.float32)

    def one_seq(carry, item):
        acc_qkv, acc_out, acc_in, acc_down, acc_g1, acc_g2, acc_g3, acc_g4 = carry
        tokens, pos, dy = item
        scale_one = rms_scale(tokens)
        normed_one = tokens * scale_one
        xn = (normed_one * gain_one).astype(jnp.bfloat16)
        query_key_value = fdot(xn, w_qkv).astype(jnp.bfloat16)
        query_matrix = query_key_value[:, :query_width].reshape(SEQUENCE_LENGTH, KEY_VALUE_HEADS, group_share, HEAD_SIZE).astype(jnp.float32)
        key_matrix = query_key_value[:, query_width:query_width + key_width].reshape(SEQUENCE_LENGTH, KEY_VALUE_HEADS, HEAD_SIZE).astype(jnp.float32)
        value_matrix = query_key_value[:, query_width + key_width:].reshape(SEQUENCE_LENGTH, KEY_VALUE_HEADS, HEAD_SIZE).astype(jnp.float32)
        allowed = (pos[None, :] <= pos[:, None])[None, None, :, :]
        raw = jnp.einsum('tgrd,ugd->grtu', query_matrix, key_matrix) * qscale
        capped = CAP * jnp.tanh(raw / CAP)
        total = lax.optimization_barrier(jnp.sum(jnp.where(allowed, jnp.exp(capped), 0.0), axis=-1, keepdims=True))
        log_total = jnp.log(total)
        probs = jnp.where(allowed, jnp.exp(capped - log_total), 0.0)
        probs_b = probs.astype(jnp.bfloat16)
        attended_output = jnp.einsum('grtu,ugd->tgrd', probs_b.astype(jnp.float32), value_matrix).reshape(SEQUENCE_LENGTH, query_width).astype(jnp.bfloat16)
        proj = fdot(attended_output, w_out)
        scale_two = rms_scale(proj)
        normed_two = proj * scale_two
        h_one = tokens + normed_two * gain_two
        scale_three = rms_scale(h_one)
        normed_three = h_one * scale_three
        u_in = (normed_three * gain_three).astype(jnp.bfloat16)
        gate_up = fdot(u_in, w_in)
        gate = gate_up[:, :FF]
        up_part = gate_up[:, FF:]
        hidden = (gelu_value(gate) * up_part).astype(jnp.bfloat16)
        ffn_out = fdot(hidden, w_down)
        scale_four = rms_scale(ffn_out)
        normed_four = ffn_out * scale_four
        y_seq = h_one + normed_four * gain_four
        dg4 = lax.optimization_barrier(jnp.sum(dy * normed_four, axis=0))
        d_ffn = norm_back(dy * gain_four, normed_four, scale_four).astype(jnp.bfloat16)
        d_down = fdot(hidden.T, d_ffn)
        d_hidden = fdot(d_ffn, w_down.T)
        d_gu = jnp.concatenate([d_hidden * up_part * gelu_slope(gate), d_hidden * gelu_value(gate)], axis=1).astype(jnp.bfloat16)
        d_inw = fdot(u_in.T, d_gu)
        d_u = fdot(d_gu, w_in.T)
        dg3 = lax.optimization_barrier(jnp.sum(d_u * normed_three, axis=0))
        d_h1 = dy + norm_back(d_u * gain_three, normed_three, scale_three)
        dg2 = lax.optimization_barrier(jnp.sum(d_h1 * normed_two, axis=0))
        d_proj = norm_back(d_h1 * gain_two, normed_two, scale_two).astype(jnp.bfloat16)
        d_outw = fdot(attended_output.T, d_proj)
        attention_gradient = fdot(d_proj, w_out.T).astype(jnp.bfloat16)
        head_attention_gradient = attention_gradient.reshape(SEQUENCE_LENGTH, KEY_VALUE_HEADS, group_share, HEAD_SIZE).astype(jnp.float32)
        attention_head = attended_output.reshape(SEQUENCE_LENGTH, KEY_VALUE_HEADS, group_share, HEAD_SIZE).astype(jnp.float32)
        d_probs = jnp.einsum('tgrd,ugd->grtu', head_attention_gradient, value_matrix)
        softmax_delta = jnp.einsum('jkcs,jkcs->kcj', head_attention_gradient, attention_head)
        d_score = (probs * (d_probs - softmax_delta[..., None]) * (1.0 - (capped / CAP) ** 2) * qscale).astype(jnp.bfloat16).astype(jnp.float32)
        d_query = jnp.einsum('grtu,ugd->tgrd', d_score, key_matrix).reshape(SEQUENCE_LENGTH, query_width)
        d_keys = jnp.einsum('grtu,tgrd->ugd', d_score, query_matrix).reshape(SEQUENCE_LENGTH, key_width)
        d_values = jnp.einsum('grtu,tgrd->ugd', probs_b.astype(jnp.float32), head_attention_gradient).reshape(SEQUENCE_LENGTH, key_width)
        d_qkv = jnp.concatenate([d_query, d_keys, d_values], axis=1).astype(jnp.bfloat16)
        d_qkvw = fdot(xn.T, d_qkv)
        d_xn = fdot(d_qkv, w_qkv.T)
        dg1 = lax.optimization_barrier(jnp.sum(d_xn * normed_one, axis=0))
        dx_seq = d_h1 + norm_back(d_xn * gain_one, normed_one, scale_one)
        carry = (acc_qkv + d_qkvw, acc_out + d_outw, acc_in + d_inw, acc_down + d_down, acc_g1 + dg1, acc_g2 + dg2, acc_g3 + dg3, acc_g4 + dg4)
        return (carry, (y_seq, dx_seq))
    init = (jnp.zeros((D, query_width + 2 * key_width), jnp.float32), jnp.zeros((query_width, D), jnp.float32), jnp.zeros((D, 2 * FF), jnp.float32), jnp.zeros((FF, D), jnp.float32), jnp.zeros((D,), jnp.float32), jnp.zeros((D,), jnp.float32), jnp.zeros((D,), jnp.float32), jnp.zeros((D,), jnp.float32))
    grads, outs = lax.scan(one_seq, init, (activations, positions, cotangent))
    y_all, dx_all = outs
    return (y_all, dx_all, grads[0], grads[1], grads[2], grads[3], grads[4], grads[5], grads[6], grads[7])
```

```python
import math

import jax
import jax.numpy as jnp
from jax import lax
from jax.sharding import PartitionSpec as P

QUERY_HEADS = 8
KEY_VALUE_HEADS = 4
HEAD_SIZE = 256

EPS = 1e-06
CAP = 50.0
GELU_C = math.sqrt(2.0 / math.pi)
AXES = ("grp", "rep")
F32 = jnp.float32
BF16 = jnp.bfloat16


def rms_scale(v):
    return lax.rsqrt(jnp.mean(v * v, axis=-1, keepdims=True) + EPS)


def norm_back(grad_n, normed, scale):
    return scale * (grad_n - normed * jnp.mean(grad_n * normed, axis=-1, keepdims=True))


def gelu_both(v):
    tanh_val = jnp.tanh(GELU_C * (v + 0.044715 * v * v * v))
    value = 0.5 * v * (1.0 + tanh_val)
    slope = 0.5 * (1.0 + tanh_val) + 0.5 * v * (1.0 - tanh_val * tanh_val) * GELU_C * (
        1.0 + 3.0 * 0.044715 * v * v
    )
    return value, slope


def fdot(a, b):
    return jnp.dot(a, b, preferred_element_type=F32)


def left_dot(a, b):
    return lax.dot_general(a, b, (((0,), (0,)), ((), ())), preferred_element_type=F32)


def right_dot(a, b):
    return lax.dot_general(a, b, (((1,), (1,)), ((), ())), preferred_element_type=F32)


def tie(value, *after):
    return lax.optimization_barrier((value,) + after)[0]


class Net:
    def __init__(self, groups, replicas):
        self.groups, self.replicas = groups, replicas
        self.line = replicas // 2
        self.g = lax.axis_index("grp")
        self.r = lax.axis_index("rep")
        self.core = self.r % 2
        self.z = self.r // 2

    def to_group(self, value, k):
        pairs = [
            (g * self.replicas + r, (g ^ k) * self.replicas + r)
            for g in range(self.groups)
            for r in range(self.replicas)
        ]
        return lax.ppermute(value, AXES, pairs)

    def to_rep(self, value, k):
        pairs = [
            (g * self.replicas + r, g * self.replicas + (r ^ k))
            for g in range(self.groups)
            for r in range(self.replicas)
        ]
        return lax.ppermute(value, AXES, pairs)

    def along_line(self, value, moves):
        pairs = [
            ((g * self.line + a) * 2 + c, (g * self.line + b) * 2 + c)
            for g in range(self.groups)
            for a, b in moves
            for c in range(2)
        ]
        return lax.ppermute(value, AXES, pairs)

    def gather(self, block):
        if self.groups != 4:
            return [block] + [self.to_group(block, k) for k in range(1, self.groups)]
        half = block.shape[0] // 2
        one = self.to_group(block, 1)
        two = self.to_group(block, 2)
        low = self.to_group(one[:half], 2)
        high = self.to_group(two[half:], 1)
        return [block, one, two, jnp.concatenate([low, high], axis=0)]

    def scatter_sum(self, blocks):
        if self.groups != 4:
            total = blocks[0].astype(F32)
            for k in range(1, self.groups):
                total = total + self.to_group(blocks[k].astype(BF16), k).astype(F32)
            return total
        half = blocks[0].shape[0] // 2
        far = blocks[3].astype(BF16)
        low = self.to_group(far[:half], 2).astype(F32)
        high = self.to_group(far[half:], 1).astype(F32)
        one = jnp.concatenate(
            [(blocks[1][:half].astype(F32) + low).astype(BF16), blocks[1][half:].astype(BF16)], axis=0
        )
        two = jnp.concatenate(
            [blocks[2][:half].astype(BF16), (blocks[2][half:].astype(F32) + high).astype(BF16)], axis=0
        )
        return (
            blocks[0].astype(F32)
            + self.to_group(one, 1).astype(F32)
            + self.to_group(two, 2).astype(F32)
        )

    def exchange(self, blocks):
        return [blocks[0]] + [self.to_group(blocks[k], k) for k in range(1, self.groups)]

    def spread(self, pieces):
        out = [(self.r % 4, pieces)]
        far = self.to_rep(pieces, 2)
        out.append((self.r % 4 ^ 2, far))
        out.append((self.r % 4 ^ 1, self.to_rep(pieces, 1)))
        out.append((self.r % 4 ^ 3, self.to_rep(far, 1)))
        return out

    def sum_line(self, value):
        if self.line == 1:
            return value
        last = self.line - 1
        mid = self.line // 2
        for i in range(mid - 1):
            got = self.along_line(value, [(i, i + 1), (last - i, last - i - 1)])
            value = (value.astype(F32) + got.astype(F32)).astype(BF16)
        got = self.along_line(value, [(mid - 1, mid), (mid, mid - 1)])
        value = (value.astype(F32) + got.astype(F32)).astype(BF16)
        for i in range(mid - 2, -1, -1):
            got = self.along_line(value, [(i + 1, i), (last - i - 1, last - i)])
            ends = (self.z <= i) | (self.z >= last - i)
            value = jnp.where(ends, got, value)
        return value

    def sum_rep(self, value):
        k = 1
        while k < self.replicas:
            value = value + self.to_rep(value, k)
            k *= 2
        return value


def head_columns(net, rows, j, per_group):
    query_width = QUERY_HEADS * HEAD_SIZE
    key_width = KEY_VALUE_HEADS * HEAD_SIZE
    heads, kv_heads, share = per_group
    kv = j // share
    return jnp.concatenate(
        [
            lax.dynamic_slice_in_dim(rows, j * (heads * HEAD_SIZE), heads * HEAD_SIZE, 1),
            lax.dynamic_slice_in_dim(rows, query_width + kv * (kv_heads * HEAD_SIZE), kv_heads * HEAD_SIZE, 1),
            lax.dynamic_slice_in_dim(
                rows, query_width + key_width + kv * (kv_heads * HEAD_SIZE), kv_heads * HEAD_SIZE, 1
            ),
        ],
        axis=1,
    )


def ff_columns(rows, j, width):
    total = rows.shape[1] // 2
    return jnp.concatenate(
        [
            lax.dynamic_slice_in_dim(rows, j * width, width, 1),
            lax.dynamic_slice_in_dim(rows, total + j * width, width, 1),
        ],
        axis=1,
    )


def columns_of_all(net, shard, pick, after=()):
    rows = shard.shape[0]
    quarter = rows // 4
    mine = lax.dynamic_slice_in_dim(shard, (net.r % 4) * quarter, quarter, 0)
    if after:
        mine = tie(mine, *after)
    got = jnp.stack([net.to_group(pick(mine, net.g ^ k), k) for k in range(1, net.groups)])
    own = pick(shard, net.g)
    full = jnp.zeros((net.groups, rows, own.shape[1]), shard.dtype)
    full = lax.dynamic_update_slice(full, own[None], (net.g, 0, 0))
    for place, part in net.spread(got):
        for k in range(1, net.groups):
            full = lax.dynamic_update_slice(full, part[k - 1 : k], (net.g ^ k, place * quarter, 0))
    return full.reshape(net.groups * rows, own.shape[1])


def rows_of_all(net, shard, after=()):
    rows = shard.shape[0]
    quarter = rows // 4
    mine = lax.dynamic_slice_in_dim(shard, (net.r % 4) * quarter, quarter, 0)
    if after:
        mine = tie(mine, *after)
    got = jnp.stack(net.gather(mine)[1:])
    full = jnp.zeros((net.groups, rows, shard.shape[1]), shard.dtype)
    full = lax.dynamic_update_slice(full, shard[None], (0, 0, 0))
    for place, part in net.spread(got):
        full = lax.dynamic_update_slice(full, part, (1, place * quarter, 0))
    return full.reshape(net.groups * rows, shard.shape[1])


def split_cores(net, halves):
    mine = lax.dynamic_index_in_dim(halves, net.core, 0, keepdims=False)
    other = lax.dynamic_index_in_dim(halves, 1 - net.core, 0, keepdims=False)
    got = net.to_rep(other, 1)
    return (mine.astype(F32) + got.astype(F32)).astype(BF16)


def join_cores(net, half):
    other = net.to_rep(half, 1)
    first = net.core == 0
    return (
        jnp.where(first, half, other).astype(F32),
        jnp.where(first, other, half).astype(F32),
    )


def attention_forward(queries, keys, values, allowed, qscale):
    tokens, heads, size = queries.shape
    kv_heads = keys.shape[1]
    q = queries.reshape(tokens, kv_heads, heads // kv_heads, size)
    raw = jnp.einsum("tgrd,ugd->grtu", q, keys, preferred_element_type=F32) * qscale
    capped = CAP * jnp.tanh(raw / CAP)
    weights = jnp.where(allowed, jnp.exp(capped), 0.0)
    total = jnp.sum(weights, axis=-1, keepdims=True)
    log_total = jnp.log(total)
    probs_b = jnp.where(allowed, jnp.exp(capped - log_total), 0.0).astype(BF16)
    attended = jnp.einsum("grtu,ugd->tgrd", probs_b, values, preferred_element_type=F32)
    return attended.astype(BF16).reshape(tokens, heads * size), log_total


def attention_backward(queries, keys, values, allowed, qscale, log_total, attended, d_attended):
    tokens, heads, size = queries.shape
    kv_heads = keys.shape[1]
    shape = (tokens, kv_heads, heads // kv_heads, size)
    q = queries.reshape(shape)
    att = attended.reshape(shape)
    d_att = d_attended.reshape(shape)
    raw = jnp.einsum("tgrd,ugd->grtu", q, keys, preferred_element_type=F32) * qscale
    capped = CAP * jnp.tanh(raw / CAP)
    probs = jnp.where(allowed, jnp.exp(capped - log_total), 0.0)
    probs_b = probs.astype(BF16)
    d_probs = jnp.einsum("tgrd,ugd->grtu", d_att, values, preferred_element_type=F32)
    delta = jnp.einsum("tgrd,tgrd->grt", d_att, att, preferred_element_type=F32)
    d_score = (
        probs * (d_probs - delta[..., None]) * (1.0 - (capped / CAP) ** 2) * qscale
    ).astype(BF16)
    d_query = jnp.einsum("grtu,ugd->tgrd", d_score, keys, preferred_element_type=F32)
    d_key = jnp.einsum("grtu,tgrd->ugd", d_score, q, preferred_element_type=F32)
    d_value = jnp.einsum("grtu,tgrd->ugd", probs_b, d_att, preferred_element_type=F32)
    return (
        d_query.reshape(tokens, heads * size),
        d_key.reshape(tokens, kv_heads * size),
        d_value.reshape(tokens, kv_heads * size),
    )


def body(
    activations,
    positions,
    w_qkv,
    w_out,
    w_in,
    w_down,
    gain_attn_in,
    gain_attn_out,
    gain_ffn_in,
    gain_ffn_out,
    cotangent,
):
    sequences, rows, width = activations.shape
    groups, replicas = lax.axis_size("grp"), lax.axis_size("rep")
    net = Net(groups, replicas)
    g = net.g
    qscale = 1.0 / math.sqrt(HEAD_SIZE)
    heads = QUERY_HEADS // groups
    kv_heads = max(1, KEY_VALUE_HEADS // groups)
    share = max(1, groups // KEY_VALUE_HEADS)
    per_group = (heads, kv_heads, share)
    head_width = heads * HEAD_SIZE
    kv_width = kv_heads * HEAD_SIZE
    ff = w_in.shape[1] // 2
    ff_part = ff // groups
    d_rows = w_qkv.shape[0]
    assert sequences == 1

    gains_own = jnp.stack([gain_attn_in, gain_attn_out, gain_ffn_in, gain_ffn_out])
    gains = jnp.zeros((groups, 4, d_rows), BF16)
    for k, part in enumerate([gains_own] + [net.to_group(gains_own, k) for k in range(1, groups)]):
        gains = lax.dynamic_update_slice(gains, part[None], (g ^ k, 0, 0))
    gains = gains.transpose(1, 0, 2).reshape(4, width).astype(F32)
    gain_one, gain_two, gain_three, gain_four = gains[0], gains[1], gains[2], gains[3]

    tokens = activations.reshape(rows, width)
    scale_one = rms_scale(tokens)
    normed_one = tokens * scale_one
    xn = (normed_one * gain_one).astype(BF16)
    xn_blocks = net.gather(xn)
    wqkv = columns_of_all(net, w_qkv, lambda rows_, j: head_columns(net, rows_, j, per_group))
    wout = rows_of_all(net, w_out, after=(xn_blocks[1], xn_blocks[2]))
    win = columns_of_all(
        net, w_in, lambda rows_, j: ff_columns(rows_, j, ff_part), after=(xn_blocks[1], xn_blocks[2])
    )

    xn_all = jnp.concatenate(xn_blocks, axis=0)
    span = rows * groups
    qkv = fdot(xn_all, wqkv).astype(BF16)
    queries = qkv[:, :head_width].reshape(span, heads, HEAD_SIZE)
    keys = qkv[:, head_width : head_width + kv_width].reshape(span, kv_heads, HEAD_SIZE)
    values = qkv[:, head_width + kv_width :].reshape(span, kv_heads, HEAD_SIZE)
    pos = jnp.concatenate(
        [lax.dynamic_slice_in_dim(positions[0], (g ^ k) * rows, rows, 0) for k in range(groups)]
    )
    allowed = pos[None, :] <= pos[:, None]
    attended, log_total = attention_forward(queries, keys, values, allowed, qscale)
    att_mine = jnp.concatenate(
        net.exchange([attended[k * rows : (k + 1) * rows] for k in range(groups)]), axis=1
    )
    proj = fdot(att_mine, wout)
    scale_two = rms_scale(proj)
    normed_two = proj * scale_two
    h_one = tokens + normed_two * gain_two

    scale_three = rms_scale(h_one)
    normed_three = h_one * scale_three
    u_in = (normed_three * gain_three).astype(BF16)
    u_all = jnp.concatenate(net.gather(u_in), axis=0)
    gate_up = fdot(u_all, win)
    gate = gate_up[:, :ff_part]
    up_part = gate_up[:, ff_part:]
    gate_act, gate_slope = gelu_both(gate)
    hidden = (gate_act * up_part).astype(BF16)
    f_blocks = [fdot(hidden[k * rows : (k + 1) * rows], w_down) for k in range(groups)]
    ffn_out = net.scatter_sum(f_blocks)
    scale_four = rms_scale(ffn_out)
    normed_four = ffn_out * scale_four
    y_rows = h_one + normed_four * gain_four

    d_out = cotangent.reshape(rows, width)
    d_gain_four = jnp.sum(d_out * normed_four, axis=0)
    d_ffn = norm_back(d_out * gain_four, normed_four, scale_four).astype(BF16)
    d_ffn_all = jnp.concatenate(net.gather(d_ffn), axis=0)
    d_hidden = right_dot(d_ffn_all, w_down)
    d_gate = (d_hidden * up_part * gate_slope).astype(BF16)
    d_up = (d_hidden * gate_act).astype(BF16)
    d_gu = jnp.concatenate([d_gate, d_up], axis=1)
    du_blocks = [right_dot(d_gu[k * rows : (k + 1) * rows], win) for k in range(groups)]
    d_u = net.scatter_sum(du_blocks)
    d_down = left_dot(hidden, d_ffn_all).astype(BF16)
    d_in_gate = left_dot(u_all, d_gate).astype(BF16)
    d_in_up = left_dot(u_all, d_up).astype(BF16)
    d_gain_three = jnp.sum(d_u * normed_three, axis=0)
    d_h_one = d_out + norm_back(d_u * gain_three, normed_three, scale_three)

    d_gain_two = jnp.sum(d_h_one * normed_two, axis=0)
    d_proj = norm_back(d_h_one * gain_two, normed_two, scale_two).astype(BF16)
    d_att_mine = right_dot(d_proj, wout).astype(BF16)
    d_attended = jnp.concatenate(
        net.exchange([d_att_mine[:, k * head_width : (k + 1) * head_width] for k in range(groups)]),
        axis=0,
    )
    d_proj_all = jnp.concatenate(net.gather(d_proj), axis=0)
    d_outw = left_dot(attended, d_proj_all).astype(BF16)
    d_query, d_key, d_value = attention_backward(
        queries, keys, values, allowed, qscale, log_total, attended, d_attended
    )
    if share > 1:
        k = 1
        while k < share:
            d_key = d_key + net.to_group(d_key, k)
            d_value = d_value + net.to_group(d_value, k)
            k *= 2
        owner = g % share == 0
        d_key = jnp.where(owner, d_key, 0.0)
        d_value = jnp.where(owner, d_value, 0.0)
    d_qkv = jnp.concatenate([d_query, d_key, d_value], axis=1).astype(BF16)
    dxn_blocks = [right_dot(d_qkv[k * rows : (k + 1) * rows], wqkv) for k in range(groups)]
    d_xn = net.scatter_sum(dxn_blocks)
    d_qkvw = left_dot(xn_all, d_qkv).astype(BF16)
    d_gain_one = jnp.sum(d_xn * normed_one, axis=0)
    dx_rows = d_h_one + norm_back(d_xn * gain_one, normed_one, scale_one)

    def by_rows(grad, parts):
        half = grad.shape[0] // 2
        piece = half // parts
        mine = split_cores(net, grad.reshape(2, half, grad.shape[1]))
        return [net.sum_line(mine[i * piece : (i + 1) * piece]) for i in range(parts)]

    def rows_out(pieces):
        pairs = [join_cores(net, piece) for piece in pieces]
        return jnp.concatenate([p[0] for p in pairs] + [p[1] for p in pairs], axis=0)

    def to_owner(grad):
        n = grad.shape[1]
        half = d_rows // 2
        halves = grad.reshape(groups, 2, half, n).transpose(1, 0, 2, 3)
        mine = split_cores(net, halves)
        blocks = [lax.dynamic_index_in_dim(mine, g ^ k, 0, keepdims=False) for k in range(groups)]
        return net.exchange(blocks)

    def place_columns(blocks, total):
        n = blocks[0].shape[1]
        full = jnp.zeros((blocks[0].shape[0], total), BF16)
        for k, block in enumerate(blocks):
            full = lax.dynamic_update_slice(full, block, (0, (g ^ k) * n))
        return full

    def in_parts(value, parts):
        piece = value.shape[0] // parts
        return [value[i * piece : (i + 1) * piece] for i in range(parts)]

    def columns_out(half, parts):
        return rows_out([net.sum_line(piece) for piece in in_parts(half, parts)])

    out_down = rows_out(by_rows(d_down, 2))
    out_gate = columns_out(place_columns(to_owner(d_in_gate), ff), 2)
    out_up = columns_out(place_columns(to_owner(d_in_up), ff), 2)
    out_in = jnp.concatenate([out_gate, out_up], axis=1)
    out_outw = rows_out(by_rows(d_outw, 1))
    qkv_blocks = to_owner(d_qkvw)
    query_width = QUERY_HEADS * HEAD_SIZE
    key_width = KEY_VALUE_HEADS * HEAD_SIZE
    half_qkv = jnp.zeros((d_rows // 2, query_width + 2 * key_width), BF16)
    for k, block in enumerate(qkv_blocks):
        j = g ^ k
        half_qkv = lax.dynamic_update_slice(half_qkv, block[:, :head_width], (0, j * head_width))
        for at in range(2):
            part = block[:, head_width + at * kv_width : head_width + (at + 1) * kv_width]
            place = (0, query_width + at * key_width + (j // share) * kv_width)
            if share > 1:
                part = part + lax.dynamic_slice(half_qkv, place, part.shape)
            half_qkv = lax.dynamic_update_slice(half_qkv, part, place)
    out_qkv = columns_out(half_qkv, 2)

    def gain_sum(grads):
        n = grads.shape[0]
        parts = grads.reshape(n, groups, d_rows).transpose(1, 0, 2)
        total = lax.dynamic_index_in_dim(parts, g, 0, keepdims=False)
        for k in range(1, groups):
            total = total + net.to_group(lax.dynamic_index_in_dim(parts, g ^ k, 0, keepdims=False), k)
        return net.sum_rep(total)

    late = gain_sum(jnp.stack([d_gain_two, d_gain_three, d_gain_four]))
    first = gain_sum(d_gain_one[None])

    return (
        y_rows.reshape(sequences, rows, width),
        dx_rows.reshape(sequences, rows, width),
        out_qkv,
        out_outw,
        out_in,
        out_down,
        first[0],
        late[0],
        late[1],
        late[2],
    )


def solution(mesh):
    return jax.shard_map(
        body,
        mesh=mesh,
        in_specs=(
            P("rep", "grp", None),
            P("rep", None),
            P("grp", None),
            P("grp", None),
            P("grp", None),
            P("grp", None),
            P("grp"),
            P("grp"),
            P("grp"),
            P("grp"),
            P("rep", "grp", None),
        ),
        out_specs=(
            P("rep", "grp", None),
            P("rep", "grp", None),
            P("grp", None),
            P("grp", None),
            P("grp", None),
            P("grp", None),
            P("grp"),
            P("grp"),
            P("grp"),
            P("grp"),
        ),
        check_vma=False,
    )
```
